512 devices in a mesh: freq: 32 (over z_lo, x), src: 2 (over z_hi), rcv: 8 (over y, core).
Axes of the slice: x: 4, y: 4, z: 16 (z_hi: 2, z_lo: 8; z = z_hi * 8 + z_lo), core: 2. Of those that a mesh axis runs over, the one named last changes fastest.
Arguments:
- traces: float32 [1024, 1024, 256], P(('src', 'freq'), 'rcv'), may hold values from -6 to 6
Outputs:
- multiples: float32 [2, 96, 1024, 1024], P(None, 'freq', 'src', 'rcv')
The draws below stay inside these ranges and needn't reach their ends.
All inputs are finite; a program needn't handle non-finite values.
Results may differ from the reference program's by a relative error of at most 0.000098.
Values sent between devices are 32-bit elements; how exact they have to be, the bound alone decides.
A program may use at most 64 MiB of HBM per device.

```python
import math
import jax
import jax.numpy as jnp
from jax import lax

N = 1024
NT = 256
NF = 96


def levels(rng, dims, split, least, high):
    loudness, own = 1.0, jax.random.fold_in(rng, 6)
    for dim, parts in split:
        heights = jnp.exp(jax.random.uniform(jax.random.fold_in(own, dim), (parts,), jnp.float32, least / len(split), high / len(split)))
        loudness = loudness * jnp.repeat(heights, dims[dim] // parts).reshape([-1 if axis == dim else 1 for axis in range(len(dims))])
    return loudness


def centred(own_key, dims, spread, limit, pieces=(), kind=jnp.bfloat16):
    factor_of = levels(own_key, dims, pieces, -0.22, 0.18) if pieces else 1.0
    values = jax.random.normal(own_key, dims, jnp.float32) * spread * factor_of
    return jnp.minimum(jnp.maximum(values, -limit), limit).astype(kind)


def setup_inputs(seed: int = 0) -> dict:
    key_of = jax.random.split(jax.random.key(seed), 2)
    return {
        "traces": centred(key_of[0], (N, N, NT), 1.0, 6.0, ((0, 64), (1, 8)), jnp.float32),
    }


def dft_matrix(n_time, n_freq):
    times = jnp.arange(n_time, dtype=jnp.int32)
    bins = jnp.arange(n_freq, dtype=jnp.int32)
    phase = times[:, None] * bins[None, :] % n_time
    angle = phase.astype(jnp.float32) * (2.0 * math.pi / n_time)
    both = jnp.stack([jnp.cos(angle), -jnp.sin(angle)], axis=-1)
    return both.reshape(n_time, 2 * n_freq) * (1.0 / math.sqrt(n_time))

def partial_dot(left, right):
    return jnp.dot(left, right, precision=lax.Precision.HIGHEST, preferred_element_type=jnp.float32)

def reference(traces):
    dft_table = dft_matrix(NT, NF)
    block_size = N // 16
    grouped = traces.reshape(N // block_size, block_size * N, NT)

    def transform(source_block):
        return jnp.dot(source_block, dft_table, precision=lax.Precision.HIGHEST, preferred_element_type=jnp.float32)
    spectra = lax.map(transform, grouped).reshape(N, N, NF, 2)
    spectra_re = jnp.transpose(spectra[:, :, :, 0], (2, 0, 1))
    spectra_im = jnp.transpose(spectra[:, :, :, 1], (2, 0, 1))

    def multiply(pair):
        left_re, left_im = pair
        real_part = partial_dot(left_re, left_re) - partial_dot(left_im, left_im)
        imag_part = partial_dot(left_re, left_im) + partial_dot(left_im, left_re)
        return (real_part, imag_part)
    out_re, out_im = lax.map(multiply, (spectra_re, spectra_im))
    scale = -1.0 / math.sqrt(N)
    return jnp.stack([out_re, out_im]) * scale
```

```python
import math

import jax
import jax.numpy as jnp
import ml_dtypes
import numpy as np
from jax import lax
from jax.experimental import pallas as pl
from jax.experimental.pallas import tpu as pltpu
from jax.sharding import PartitionSpec as P

N = 1024
NT = 256
NF = 96
FPD = 3
PLANES = 2 * FPD
BLOCK = 16 * PLANES
GROUP = 4 * BLOCK
HALF = 8 * GROUP
ROW = 2 * HALF
MESH = pl.DeviceIdType.MESH
SCALE = -1.0 / math.sqrt(N)
ORDER = [(0, i) for i in range(1, 8)] + [(1, i) for i in range(1, 9)]
XPART = 4


def split(x):
    hi = x.astype(jnp.bfloat16)
    return hi, (x - hi.astype(jnp.float32)).astype(jnp.bfloat16)


def dft_table():
    phase = np.arange(NF)[:, None] * np.arange(NT)[None, :] % NT
    angle = phase * (2.0 * math.pi / NT)
    both = np.stack([np.cos(angle), -np.sin(angle)], axis=1)
    both = (both.reshape(2 * NF, NT) / math.sqrt(NT)).astype(np.float32)
    hi = both.astype(ml_dtypes.bfloat16)
    lo = (both - hi.astype(np.float32)).astype(ml_dtypes.bfloat16)
    return np.stack([hi, lo])


def near(i, at, count):
    sides = jnp.minimum(at, count - 1 - at)
    both = i <= 2 * sides
    far = jnp.where(both, (i + 1) // 2, i - sides)
    up = jnp.where(both, i % 2 == 1, at < count // 2)
    return jnp.where(up, far, -far)


def across(i, at):
    if i == 8:
        return 8
    up_first, down_first = 8 - at, at + 1
    single = jnp.abs(2 * at - 7)
    one = i <= single
    j = i - single
    far = jnp.where(
        one,
        jnp.minimum(up_first, down_first) + i - 1,
        jnp.maximum(up_first, down_first) + (j - 1) // 2,
    )
    up = jnp.where(one, at >= 4, j % 2 == 1)
    return jnp.where(up, far, -far)


def kernel(
    traces,
    table,
    out,
    xin,
    spec,
    big,
    ahi,
    alo,
    bhi,
    blo,
    xsem,
    lsem,
    zsend,
    ysend,
    csend,
    zsem,
    ysem,
    csem,
):
    f = lax.axis_index("freq")
    h = lax.axis_index("src")
    r = lax.axis_index("rcv")
    x, zl = lax.rem(f, 4), f // 4
    y, c = r // 2, lax.rem(r, 2)
    z = h * 8 + zl

    def device(dx, dy, dz, dc):
        x2, y2 = lax.rem(x + dx, 4), lax.rem(y + dy, 4)
        z2, c2 = lax.rem(z + dz + 16, 16), lax.rem(c + dc, 2)
        return (lax.rem(z2, 8) * 4 + x2, z2 // 8, y2 * 2 + c2)

    def rows(start, n):
        return big.at[pl.ds(pl.multiple_of(start, BLOCK), n)]

    def wait(ref, sem):
        pltpu.make_async_copy(ref, ref, sem).wait()

    def send(src, dst, ssem, rsem, to):
        pltpu.make_async_remote_copy(
            src, dst, ssem, rsem, device_id=to, device_id_type=MESH
        ).start()

    barrier = pltpu.get_barrier_semaphore()
    peers = [(dx, 0, dz, 0) for dz in range(16) for dx in range(4) if dx or dz]
    peers += [(0, dy, 0, 0) for dy in (1, 2, 3)] + [(0, 0, 0, 1)]
    per = 2048 // XPART
    loads = [
        pltpu.make_async_copy(
            traces.at[pl.ds(k * per, per)], xin.at[pl.ds(k * per, per)], xsem.at[k]
        )
        for k in range(XPART)
    ]
    with jax.named_scope("signal"):
        for load in loads:
            load.start()
        for p in peers:
            pl.semaphore_signal(
                barrier, inc=1, device_id=device(*p), device_id_type=MESH
            )
    with jax.named_scope("dft"):
        thi, tlo = table[0], table[1]
        dims = (((1,), (1,)), ((), ()))
        for k in range(8):
            if k % (8 // XPART) == 0:
                loads[k // (8 // XPART)].wait()
            xhi, xlo = split(xin[pl.ds(k * 256, 256), :])
            got = sum(
                lax.dot_general(a, b, dims, preferred_element_type=jnp.float32)
                for a, b in ((thi, xhi), (tlo, xhi), (thi, xlo))
            )
            for i in range(2):
                spec[pl.ds(2 * k + i, 2 * NF, stride=16), :] = got[
                    :, i * 128 : (i + 1) * 128
                ]
    with jax.named_scope("barrier"):
        pl.semaphore_wait(barrier, len(peers))

    with jax.named_scope("issue"):
        mine = (z * 4 + x) * BLOCK

        def zcopy(dz, dx):
            to = device(dx, 0, dz, 0)
            src = spec.at[pl.ds(pl.multiple_of(to[0] * BLOCK, BLOCK), BLOCK)]
            send(src, rows(mine, BLOCK), zsend, zsem.at[z], to)

        own = pltpu.make_async_copy(
            spec.at[pl.ds(pl.multiple_of(f * BLOCK, BLOCK), BLOCK)],
            rows(mine, BLOCK),
            lsem,
        )
        own.start()
        for dx in (1, 2, 3):
            zcopy(0, dx)
        for kind, i in ORDER:
            dz = across(i, zl) if kind else near(i, zl, 8)
            for dx in range(4):
                zcopy(dz, dx)
        own.wait()

    def place(i):
        return zl + (near(i, zl, 8) if i else 0)

    def pass_on(i):
        at = place(i)
        for dy in (1, 3, 2):
            q = lax.rem(y - dy + 4, 4) * 2 + c
            ref = rows(ROW + q * HALF + at * GROUP, GROUP)
            wait(ref, ysem.at[(dy - 1) * 8 + at])
            send(ref, ref, csend, csem.at[dy * 8 + at], device(0, 0, 0, 1))

    for i in range(8):
        at = place(i)
        src = rows((h * 8 + at) * GROUP, GROUP)
        dst = rows(ROW + r * HALF + at * GROUP, GROUP)
        with jax.named_scope(f"own{i}"):
            wait(
                rows((h * 8 + at) * GROUP, GROUP if i else GROUP - BLOCK),
                zsem.at[h * 8 + at],
            )
        with jax.named_scope(f"fwd{i}"):
            for dy in (1, 3, 2):
                send(src, dst, ysend, ysem.at[(dy - 1) * 8 + at], device(0, dy, 0, 0))
            send(src, dst, csend, csem.at[at], device(0, 0, 0, 1))
        if i:
            with jax.named_scope(f"pass{i - 1}"):
                pass_on(i - 1)
    with jax.named_scope("pass7"):
        pass_on(7)
    with jax.named_scope("core"):
        for dy in range(4):
            q = lax.rem(y - dy + 4, 4) * 2 + 1 - c
            for at in range(8):
                wait(rows(ROW + q * HALF + at * GROUP, GROUP), csem.at[dy * 8 + at])

    def load(start):
        return big[pl.ds(pl.multiple_of(start, 16), 16), :]

    def chunk(q, first):
        base = jnp.where(q == r, h * HALF, ROW + q * HALF)

        def left(g, carry):
            at = pl.ds(pl.multiple_of(g * 16, 16), 16)
            for k in range(FPD):
                for part in range(2):
                    hi, lo = split(load(base + g * BLOCK + (2 * k + part) * 16))
                    lanes = pl.ds(part * 128, 128)
                    ahi[k, at, lanes] = hi
                    alo[k, at, lanes] = lo
            return carry

        lax.fori_loop(0, 32, left, 0)
        for b in range(8):
            for k in range(FPD):
                start = (q * 8 + b) * BLOCK + 2 * k * 16
                for part in range(2):
                    value = load(start + part * 16) * SCALE
                    for ref, v in zip((bhi, blo), split(value)):
                        ref[k, pl.ds(part * 128 + b * 16, 16), pl.ds(0, 128)] = (
                            v if part == 0 else -v
                        )
                        ref[k, pl.ds((1 - part) * 128 + b * 16, 16), pl.ds(128, 128)] = v
        return first

    def multiply(first):
        for k in range(FPD):
            for m in range(2):
                at = pl.ds(m * 256, 256)
                got = sum(
                    jnp.dot(a[k, at, :], b[k], preferred_element_type=jnp.float32)
                    for a, b in ((ahi, bhi), (alo, bhi), (ahi, blo))
                )
                for part in range(2):
                    piece = got[:, part * 128 : (part + 1) * 128]
                    if first:
                        out[part, k, at, :] = piece
                    else:
                        out[part, k, at, :] += piece

    for i in range(4):
        with jax.named_scope(f"near{i}"):
            chunk(h * 4 + i, i == 0)
            multiply(i == 0)
    mid = zl // 2
    for i in range(3, -1, -1):
        q = (1 - h) * 4 + mid + (near(i, mid, 4) if i else 0)
        with jax.named_scope(f"wait{i}"):
            for k in range(2):
                wait(rows((2 * q + k) * GROUP, GROUP), zsem.at[2 * q + k])
        with jax.named_scope(f"far{i}"):
            chunk(q, False)
            multiply(False)
    with jax.named_scope("end"):
        wait(big.at[pl.ds(0, 63 * BLOCK)], zsend)
        wait(big.at[pl.ds(0, 3 * HALF)], ysend)
        wait(big.at[pl.ds(0, 4 * HALF)], csend)


def per_device(traces):
    table = jnp.asarray(dft_table())
    vmem = pl.BlockSpec(memory_space=pltpu.VMEM)
    dma = pltpu.SemaphoreType.DMA
    return pl.pallas_call(
        kernel,
        name="multiples",
        out_shape=jax.ShapeDtypeStruct((2, FPD, N // 2, 128), jnp.float32),
        in_specs=[pl.BlockSpec(memory_space=pltpu.HBM), vmem],
        out_specs=vmem,
        scratch_shapes=[
            pltpu.VMEM((2048, NT), jnp.float32),
            pltpu.VMEM((2 * NF * 16, 128), jnp.float32),
            pltpu.VMEM((ROW + 8 * HALF, 128), jnp.float32),
            pltpu.VMEM((FPD, 512, 256), jnp.bfloat16),
            pltpu.VMEM((FPD, 512, 256), jnp.bfloat16),
            pltpu.VMEM((FPD, 256, 256), jnp.bfloat16),
            pltpu.VMEM((FPD, 256, 256), jnp.bfloat16),
            dma((XPART,)),
            dma,
            dma,
            dma,
            dma,
            dma((16,)),
            dma((24,)),
            dma((32,)),
        ],
        compiler_params=pltpu.CompilerParams(
            collective_id=0, has_side_effects=True, vmem_limit_bytes=40 << 20
        ),
    )(traces.reshape(2048, NT), table)


def solution(mesh):
    in_specs = (P(("src", "freq"), "rcv", None),)
    out_specs = P(None, "freq", "src", "rcv")
    return jax.shard_map(
        per_device, mesh=mesh, in_specs=in_specs, out_specs=out_specs, check_vma=False
    )
```

```python
import functools
import math

import jax
import jax.numpy as jnp
import ml_dtypes
import numpy as np
from jax import lax
from jax.experimental import pallas as pl
from jax.experimental.pallas import tpu as pltpu
from jax.sharding import PartitionSpec as P

N = 1024
NT = 256
NF = 96
FPD = 3
PLANES = 2 * FPD
BLOCK = 16 * PLANES
GROUP = 4 * BLOCK
HALF = 8 * GROUP
ROW = 2 * HALF
MESH = pl.DeviceIdType.MESH
SCALE = -1.0 / math.sqrt(N)
XPART = 4
RFIRST = 6


def split(x):
    hi = x.astype(jnp.bfloat16)
    return hi, (x - hi.astype(jnp.float32)).astype(jnp.bfloat16)


def dft_table():
    phase = np.arange(NF)[:, None] * np.arange(NT)[None, :] % NT
    angle = phase * (2.0 * math.pi / NT)
    both = np.stack([np.cos(angle), -np.sin(angle)], axis=1)
    both = (both.reshape(2 * NF, NT) / math.sqrt(NT)).astype(np.float32)
    hi = both.astype(ml_dtypes.bfloat16)
    lo = (both - hi.astype(np.float32)).astype(ml_dtypes.bfloat16)
    return np.stack([hi, lo])


def near(i, at, count):
    sides = jnp.minimum(at, count - 1 - at)
    both = i <= 2 * sides
    far = jnp.where(both, (i + 1) // 2, i - sides)
    up = jnp.where(both, i % 2 == 1, at < count // 2)
    return jnp.where(up, far, -far)


def kernel(
    traces,
    table,
    out,
    xin,
    tab,
    spec,
    big,
    ahi,
    alo,
    bhi,
    blo,
    whi,
    wlo,
    nhi,
    nlo,
    xsem,
    lsem,
    zsend,
    ysend,
    csend,
    zsem,
    ysem,
    csem,
    ready,
    relay,
    rsem,
    rsend,
):
    f = lax.axis_index("freq")
    h = lax.axis_index("src")
    r = lax.axis_index("rcv")
    x, zl = lax.rem(f, 4), f // 4
    y, c = r // 2, lax.rem(r, 2)
    z = h * 8 + zl

    def device(dx, dy, dz, dc):
        x2, y2 = lax.rem(x + dx, 4), lax.rem(y + dy, 4)
        z2, c2 = lax.rem(z + dz + 16, 16), lax.rem(c + dc, 2)
        return (lax.rem(z2, 8) * 4 + x2, z2 // 8, y2 * 2 + c2)

    def rows(start, n):
        return big.at[pl.ds(pl.multiple_of(start, BLOCK), n)]

    def wait(ref, sem):
        pltpu.make_async_copy(ref, ref, sem).wait()

    def send(src, dst, ssem, rsem, to):
        pltpu.make_async_remote_copy(
            src, dst, ssem, rsem, device_id=to, device_id_type=MESH
        ).start()

    barrier = pltpu.get_barrier_semaphore()
    peers = [(dx, 0, dz, 0) for dz in (1, -1, 0) for dx in range(4) if dx or dz]
    peers += [(0, dy, 0, 0) for dy in (1, 2, 3)] + [(0, 0, 0, 1)]
    per = 2048 // XPART
    loads = [
        pltpu.make_async_copy(
            traces.at[pl.ds(k * per, per)], xin.at[pl.ds(k * per, per)], xsem.at[k]
        )
        for k in range(XPART)
    ]
    loads.append(pltpu.make_async_copy(table, tab, xsem.at[XPART]))
    with jax.named_scope("signal"):
        for p in peers:
            pl.semaphore_signal(
                barrier, inc=1, device_id=device(*p), device_id_type=MESH
            )
        for load in loads[-1:] + loads[:-1]:
            load.start()
    with jax.named_scope("dft"):
        loads[XPART].wait()
        thi, tlo = tab[0], tab[1]
        dims = (((1,), (1,)), ((), ()))
        for k in range(8):
            if k % (8 // XPART) == 0:
                loads[k // (8 // XPART)].wait()
            xhi, xlo = split(xin[pl.ds(k * 256, 256), :])
            got = sum(
                lax.dot_general(a, b, dims, preferred_element_type=jnp.float32)
                for a, b in ((thi, xhi), (tlo, xhi), (thi, xlo))
            )
            for i in range(2):
                spec[pl.ds(2 * k + i, 2 * NF, stride=16), :] = got[
                    :, i * 128 : (i + 1) * 128
                ]
    with jax.named_scope("barrier"):
        pl.semaphore_wait(barrier, len(peers))

    with jax.named_scope("issue"):
        mine = (z * 4 + x) * BLOCK

        def flag(to):
            at = to[0] // 4
            farthest = zl == jnp.where(at < 4, 7, 0)
            return jnp.where((to[1] == h) & farthest, 16 + x, z)

        def zcopy(dz, dx):
            to = device(dx, 0, dz, 0)
            src = spec.at[pl.ds(pl.multiple_of(to[0] * BLOCK, BLOCK), BLOCK)]
            send(src, rows(mine, BLOCK), zsend, zsem.at[flag(to)], to)

        own = pltpu.make_async_copy(
            spec.at[pl.ds(pl.multiple_of(f * BLOCK, BLOCK), BLOCK)],
            rows(mine, BLOCK),
            lsem,
        )
        own.start()
        for dx in (1, 2, 3):
            zcopy(0, dx)

    def spread(dz):
        for dx in range(4):
            zcopy(dz, dx)

    def via(dx):
        return 4 if dx < 2 else -4

    def halfway(dx):
        to = device(dx, 0, via(dx), 0)
        goal = device(dx, 0, 8, 0)[0]
        src = spec.at[pl.ds(pl.multiple_of(goal * BLOCK, BLOCK), BLOCK)]
        slot = relay.at[pl.ds(dx * BLOCK, BLOCK)]
        send(src, slot, zsend, rsem.at[dx // 2], to)

    def onward(dx):
        to = device(0, 0, via(dx), 0)
        first = lax.rem(z - via(dx) + 16, 16)
        block = (first * 4 + lax.rem(x - dx + 4, 4)) * BLOCK
        slot = relay.at[pl.ds(dx * BLOCK, BLOCK)]
        send(slot, rows(block, BLOCK), rsend, zsem.at[first], to)

    for k in range(1, 8):
        with jax.named_scope(f"ready{k}"):
            for s in range(2):
                if k > 1:
                    pl.semaphore_wait(ready.at[s, k], 1)
                if k < 7:
                    pl.semaphore_signal(
                        ready.at[s, k + 1],
                        inc=1,
                        device_id=device(0, 0, 2 * s - 1, 0),
                        device_id_type=MESH,
                    )
            if k == RFIRST:
                for dx in range(4):
                    halfway(dx)
            spread(k)
            spread(-k)
    if RFIRST == 8:
        for dx in range(4):
            halfway(dx)
    own.wait()

    def place(i):
        return zl + (near(i, zl, 8) if i else 0)

    def pass_on(i):
        at = place(i)
        for dy in (1, 3, 2):
            q = lax.rem(y - dy + 4, 4) * 2 + c
            ref = rows(ROW + q * HALF + at * GROUP, GROUP)
            wait(ref, ysem.at[(dy - 1) * 8 + at])
            send(ref, ref, csend, csem.at[dy * 8 + at], device(0, 0, 0, 1))

    def take(i):
        at = place(i)
        src = rows((h * 8 + at) * GROUP, GROUP)
        dst = rows(ROW + r * HALF + at * GROUP, GROUP)
        with jax.named_scope(f"own{i}"):
            wait(
                rows((h * 8 + at) * GROUP, GROUP if i else GROUP - BLOCK),
                zsem.at[h * 8 + at],
            )
        for dy in (1, 3, 2):
            send(src, dst, ysend, ysem.at[(dy - 1) * 8 + at], device(0, dy, 0, 0))
        send(src, dst, csend, csem.at[at], device(0, 0, 0, 1))

    def from_core(i):
        at = place(i)
        for dy in range(4):
            q = lax.rem(y - dy + 4, 4) * 2 + 1 - c
            wait(rows(ROW + q * HALF + at * GROUP, GROUP), csem.at[dy * 8 + at])

    def load(start):
        return big[pl.ds(pl.multiple_of(start, 16), 16), :]

    def left(q, g0, n, ahi, alo):
        base = jnp.where(q == r, h * HALF, ROW + q * HALF)

        def one(j, carry):
            g = g0 + j
            at = pl.ds(pl.multiple_of(g * 16, 16), 16)
            for k in range(FPD):
                for part in range(2):
                    hi, lo = split(load(base + g * BLOCK + (2 * k + part) * 16))
                    lanes = pl.ds(part * 128, 128)
                    ahi[k, at, lanes] = hi
                    alo[k, at, lanes] = lo
            return carry

        lax.fori_loop(0, n, one, 0)

    def right(q, slot, bhi, blo):
        for b in range(8):
            for k in range(FPD):
                start = (q * 8 + b) * BLOCK + 2 * k * 16
                for part in range(2):
                    value = load(start + part * 16) * SCALE
                    for ref, v in zip((bhi, blo), split(value)):
                        i = slot * FPD + k
                        ref[i, pl.ds(part * 128 + b * 16, 16), pl.ds(0, 128)] = (
                            v if part == 0 else -v
                        )
                        ref[i, pl.ds((1 - part) * 128 + b * 16, 16), pl.ds(128, 128)] = v

    def multiply(slot, row0, sizes, ahi, alo, bhi, blo, first=False):
        for k in range(FPD):
            row = row0
            for size in sizes:
                at = pl.ds(row if isinstance(row, int) else pl.multiple_of(row, 32), size)
                i = slot * FPD + k
                got = sum(
                    jnp.dot(a[k, at, :], b[i], preferred_element_type=jnp.float32)
                    for a, b in ((ahi, bhi), (alo, bhi), (ahi, blo))
                )
                for part in range(2):
                    piece = got[:, part * 128 : (part + 1) * 128]
                    if first:
                        out[part, k, at, :] = piece
                    else:
                        out[part, k, at, :] += piece
                row = row + size

    mid = zl // 2
    swap = (zl == 2) | (zl == 4)

    def near_chunk(i):
        return h * 4 + mid + (near(i, mid, 4) if i else 0)

    def far_chunk(i):
        step = near(i, mid, 4) if i else 0
        if i in (1, 2):
            step = jnp.where(swap, near(3 - i, mid, 4), step)
        return (1 - h) * 4 + mid + step

    def arrive(q):
        for k in range(2):
            wait(rows((2 * q + k) * GROUP, GROUP), zsem.at[2 * q + k])

    def forward():
        with jax.named_scope("relay"):
            for part in range(2):
                wait(relay.at[pl.ds(part * 2 * BLOCK, 2 * BLOCK)], rsem.at[part])
                onward(2 * part)
                onward(2 * part + 1)

    for i in range(7):
        take(i)
        if i:
            with jax.named_scope(f"pass{i - 1}"):
                pass_on(i - 1)
    with jax.named_scope("pass6"):
        pass_on(6)
        for i in range(7):
            from_core(i)

    ahead = [near_chunk(i) for i in range(3)] + [far_chunk(3), far_chunk(2)]
    upper = jnp.where(zl >= 4, 1, 0)
    for slot, q in enumerate(ahead):
        with jax.named_scope(f"ahead{slot}"):
            if slot >= 3:
                arrive(q)
            left(q, upper * 4, 28, ahi, alo)
            right(q, slot, bhi, blo)
            multiply(slot, upper * 64, (224, 224), ahi, alo, bhi, blo, slot == 0)
    with jax.named_scope("core"):
        far_at = place(7)

        def piece(base, dx):
            return rows(base + far_at * GROUP + lax.rem(x - dx + 4, 4) * BLOCK, BLOCK)

        for dx in range(4):
            with jax.named_scope(f"own7{dx}"):
                src = piece(h * HALF, dx)
                wait(src, zsem.at[16 + lax.rem(x - dx + 4, 4)])
            for dy in (1, 3, 2):
                send(
                    src,
                    piece(ROW + r * HALF, dx),
                    ysend,
                    ysem.at[24 + dy * 4 + dx],
                    device(0, dy, 0, 0),
                )
            to = device(0, 0, 0, 1)
            send(src, piece(ROW + r * HALF, dx), csend, csem.at[32 + dx], to)
        forward()
        for dx in range(4):
            for dy in (1, 3, 2):
                ref = piece(ROW + (lax.rem(y - dy + 4, 4) * 2 + c) * HALF, dx)
                wait(ref, ysem.at[24 + dy * 4 + dx])
                send(ref, ref, csend, csem.at[32 + dy * 4 + dx], device(0, 0, 0, 1))
        for dx in range(4):
            for dy in (0, 1, 3, 2):
                q = lax.rem(y - dy + 4, 4) * 2 + 1 - c
                wait(piece(ROW + q * HALF, dx), csem.at[32 + dy * 4 + dx])
    with jax.named_scope("near3"):
        q = near_chunk(3)
        left(q, upper * 4, 28, ahi, alo)
        right(q, 5, bhi, blo)
        multiply(5, upper * 64, (224, 224), ahi, alo, bhi, blo)
    last = (1 - upper) * 28
    for slot, q in enumerate([*ahead, near_chunk(3)]):
        with jax.named_scope(f"late{slot}"):
            left(q, last, 4, ahi, alo)
            multiply(slot, last * 16, (64,), ahi, alo, bhi, blo, slot == 0)
    ends = ((1, ahi, alo), (0, nhi, nlo))
    for i, hi, lo in ends:
        with jax.named_scope(f"left{i}"):
            left(far_chunk(i), 0, 32, hi, lo)
    for i, hi, lo in ends:
        with jax.named_scope(f"wait{i}"):
            arrive(far_chunk(i))
        with jax.named_scope(f"far{i}"):
            right(far_chunk(i), 0, whi, wlo)
            multiply(0, 0, (256, 256), hi, lo, whi, wlo)
    with jax.named_scope("end"):
        wait(big.at[pl.ds(0, 63 * BLOCK)], zsend)
        wait(big.at[pl.ds(0, 4 * BLOCK)], rsend)
        wait(big.at[pl.ds(0, 3 * HALF)], ysend)
        wait(big.at[pl.ds(0, 4 * HALF)], csend)


def per_device(traces):
    table = jnp.asarray(dft_table())
    vmem = pl.BlockSpec(memory_space=pltpu.VMEM)
    dma = pltpu.SemaphoreType.DMA
    return pl.pallas_call(
        kernel,
        name="multiples",
        out_shape=jax.ShapeDtypeStruct((2, FPD, N // 2, 128), jnp.float32),
        in_specs=[pl.BlockSpec(memory_space=pltpu.HBM)] * 2,
        out_specs=vmem,
        scratch_shapes=[
            pltpu.VMEM((2048, NT), jnp.float32),
            pltpu.VMEM((2, 2 * NF, NT), jnp.bfloat16),
            pltpu.VMEM((2 * NF * 16, 128), jnp.float32),
            pltpu.VMEM((ROW + 8 * HALF, 128), jnp.float32),
            pltpu.VMEM((FPD, 512, 256), jnp.bfloat16),
            pltpu.VMEM((FPD, 512, 256), jnp.bfloat16),
            pltpu.VMEM((6 * FPD, 256, 256), jnp.bfloat16),
            pltpu.VMEM((6 * FPD, 256, 256), jnp.bfloat16),
            pltpu.VMEM((FPD, 256, 256), jnp.bfloat16),
            pltpu.VMEM((FPD, 256, 256), jnp.bfloat16),
            pltpu.VMEM((FPD, 512, 256), jnp.bfloat16),
            pltpu.VMEM((FPD, 512, 256), jnp.bfloat16),
            dma((XPART + 1,)),
            dma,
            dma,
            dma,
            dma,
            dma((20,)),
            dma((40,)),
            dma((48,)),
            pltpu.SemaphoreType.REGULAR((2, 8)),
            pltpu.VMEM((4 * BLOCK, 128), jnp.float32),
            dma((2,)),
            dma,
        ],
        compiler_params=pltpu.CompilerParams(
            collective_id=0, has_side_effects=True, vmem_limit_bytes=48 << 20
        ),
    )(
        pltpu.with_memory_space_constraint(traces.reshape(2048, NT), pltpu.HBM),
        pltpu.with_memory_space_constraint(table, pltpu.HBM),
    )


def solution(mesh):
    in_specs = (P(("src", "freq"), "rcv", None),)
    out_specs = P(None, "freq", "src", "rcv")
    return jax.shard_map(
        per_device, mesh=mesh, in_specs=in_specs, out_specs=out_specs, check_vma=False
    )
```

```python
import functools
import math

import jax
import jax.numpy as jnp
import ml_dtypes
import numpy as np
from jax import lax
from jax.experimental import pallas as pl
from jax.experimental.pallas import tpu as pltpu
from jax.sharding import PartitionSpec as P

N = 1024
NT = 256
NF = 96
FPD = 3
PLANES = 2 * FPD
BLOCK = 16 * PLANES
GROUP = 4 * BLOCK
HALF = 8 * GROUP
ROW = 2 * HALF
MESH = pl.DeviceIdType.MESH
SCALE = -1.0 / math.sqrt(N)
XPART = 4
RFIRST = 6


def split(x):
    hi = x.astype(jnp.bfloat16)
    return hi, (x - hi.astype(jnp.float32)).astype(jnp.bfloat16)


def dft_table():
    phase = np.arange(NF)[:, None] * np.arange(NT)[None, :] % NT
    angle = phase * (2.0 * math.pi / NT)
    both = np.stack([np.cos(angle), -np.sin(angle)], axis=1)
    both = (both.reshape(2 * NF, NT) / math.sqrt(NT)).astype(np.float32)
    hi = both.astype(ml_dtypes.bfloat16)
    lo = (both - hi.astype(np.float32)).astype(ml_dtypes.bfloat16)
    return np.stack([hi, lo])


def near(i, at, count):
    sides = jnp.minimum(at, count - 1 - at)
    both = i <= 2 * sides
    far = jnp.where(both, (i + 1) // 2, i - sides)
    up = jnp.where(both, i % 2 == 1, at < count // 2)
    return jnp.where(up, far, -far)


def kernel(
    traces,
    table,
    out,
    xin,
    tab,
    spec,
    big,
    ahi,
    alo,
    bhi,
    blo,
    whi,
    wlo,
    nhi,
    nlo,
    xsem,
    lsem,
    zsend,
    ysend,
    csend,
    zsem,
    ysem,
    csem,
    ready,
    relay,
    rsem,
    rsend,
):
    f = lax.axis_index("freq")
    h = lax.axis_index("src")
    r = lax.axis_index("rcv")
    x, zl = lax.rem(f, 4), f // 4
    y, c = r // 2, lax.rem(r, 2)
    z = h * 8 + zl

    def device(dx, dy, dz, dc):
        x2, y2 = lax.rem(x + dx, 4), lax.rem(y + dy, 4)
        z2, c2 = lax.rem(z + dz + 16, 16), lax.rem(c + dc, 2)
        return (lax.rem(z2, 8) * 4 + x2, z2 // 8, y2 * 2 + c2)

    def rows(start, n):
        return big.at[pl.ds(pl.multiple_of(start, BLOCK), n)]

    def wait(ref, sem):
        pltpu.make_async_copy(ref, ref, sem).wait()

    def send(src, dst, ssem, rsem, to):
        pltpu.make_async_remote_copy(
            src, dst, ssem, rsem, device_id=to, device_id_type=MESH
        ).start()

    barrier = pltpu.get_barrier_semaphore()
    peers = [(dx, 0, dz, 0) for dz in (1, -1, 0) for dx in range(4) if dx or dz]
    peers += [(0, dy, 0, 0) for dy in (1, 2, 3)] + [(0, 0, 0, 1)]
    per = 2048 // XPART
    loads = [
        pltpu.make_async_copy(
            traces.at[pl.ds(k * per, per)], xin.at[pl.ds(k * per, per)], xsem.at[k]
        )
        for k in range(XPART)
    ]
    loads.append(pltpu.make_async_copy(table, tab, xsem.at[XPART]))
    with jax.named_scope("signal"):
        for p in peers:
            pl.semaphore_signal(
                barrier, inc=1, device_id=device(*p), device_id_type=MESH
            )
        for load in loads[-1:] + loads[:-1]:
            load.start()
    with jax.named_scope("dft"):
        loads[XPART].wait()
        thi, tlo = tab[0], tab[1]
        dims = (((1,), (1,)), ((), ()))
        for k in range(8):
            if k % (8 // XPART) == 0:
                loads[k // (8 // XPART)].wait()
            xhi, xlo = split(xin[pl.ds(k * 256, 256), :])
            got = sum(
                lax.dot_general(a, b, dims, preferred_element_type=jnp.float32)
                for a, b in ((thi, xhi), (tlo, xhi), (thi, xlo))
            )
            for i in range(2):
                spec[pl.ds(2 * k + i, 2 * NF, stride=16), :] = got[
                    :, i * 128 : (i + 1) * 128
                ]
    with jax.named_scope("barrier"):
        pl.semaphore_wait(barrier, len(peers))

    with jax.named_scope("issue"):
        mine = (z * 4 + x) * BLOCK

        def flag(to):
            at = to[0] // 4
            farthest = zl == jnp.where(at < 4, 7, 0)
            return jnp.where((to[1] == h) & farthest, 16 + x, z)

        def zcopy(dz, dx):
            to = device(dx, 0, dz, 0)
            src = spec.at[pl.ds(pl.multiple_of(to[0] * BLOCK, BLOCK), BLOCK)]
            send(src, rows(mine, BLOCK), zsend, zsem.at[flag(to)], to)

        own = pltpu.make_async_copy(
            spec.at[pl.ds(pl.multiple_of(f * BLOCK, BLOCK), BLOCK)],
            rows(mine, BLOCK),
            lsem,
        )
        own.start()
        for dx in (1, 2, 3):
            zcopy(0, dx)

    def spread(dz):
        for dx in range(4):
            zcopy(dz, dx)

    def via(dx):
        return 4 if dx % 2 == 0 else -4

    def halfway(dx):
        to = device(dx, 0, via(dx), 0)
        goal = device(dx, 0, 8, 0)[0]
        src = spec.at[pl.ds(pl.multiple_of(goal * BLOCK, BLOCK), BLOCK)]
        slot = relay.at[pl.ds((dx % 2 * 2 + dx // 2) * BLOCK, BLOCK)]
        send(src, slot, zsend, rsem.at[dx % 2], to)

    def onward(dx):
        to = device(0, 0, via(dx), 0)
        first = lax.rem(z - via(dx) + 16, 16)
        block = (first * 4 + lax.rem(x - dx + 4, 4)) * BLOCK
        slot = relay.at[pl.ds((dx % 2 * 2 + dx // 2) * BLOCK, BLOCK)]
        send(slot, rows(block, BLOCK), rsend, zsem.at[first], to)

    for k in range(1, 8):
        with jax.named_scope(f"ready{k}"):
            for s in range(2):
                if k > 1:
                    pl.semaphore_wait(ready.at[s, k], 1)
                if k < 7:
                    pl.semaphore_signal(
                        ready.at[s, k + 1],
                        inc=1,
                        device_id=device(0, 0, 2 * s - 1, 0),
                        device_id_type=MESH,
                    )
            if k == RFIRST:
                for dx in range(4):
                    halfway(dx)
            spread(k)
            spread(-k)
    if RFIRST == 8:
        for dx in range(4):
            halfway(dx)
    own.wait()

    def place(i):
        return zl + (near(i, zl, 8) if i else 0)

    def pass_on(i):
        at = place(i)
        for dy in (1, 3, 2):
            q = lax.rem(y - dy + 4, 4) * 2 + c
            ref = rows(ROW + q * HALF + at * GROUP, GROUP)
            wait(ref, ysem.at[(dy - 1) * 8 + at])
            send(ref, ref, csend, csem.at[dy * 8 + at], device(0, 0, 0, 1))

    def take(i):
        at = place(i)
        src = rows((h * 8 + at) * GROUP, GROUP)
        dst = rows(ROW + r * HALF + at * GROUP, GROUP)
        with jax.named_scope(f"own{i}"):
            wait(
                rows((h * 8 + at) * GROUP, GROUP if i else GROUP - BLOCK),
                zsem.at[h * 8 + at],
            )
        for dy in (1, 3, 2):
            send(src, dst, ysend, ysem.at[(dy - 1) * 8 + at], device(0, dy, 0, 0))
        send(src, dst, csend, csem.at[at], device(0, 0, 0, 1))

    def from_core(i):
        at = place(i)
        for dy in range(4):
            q = lax.rem(y - dy + 4, 4) * 2 + 1 - c
            wait(rows(ROW + q * HALF + at * GROUP, GROUP), csem.at[dy * 8 + at])

    def load(start):
        return big[pl.ds(pl.multiple_of(start, 16), 16), :]

    def left(q, g0, n, ahi, alo):
        base = jnp.where(q == r, h * HALF, ROW + q * HALF)

        def one(j, carry):
            g = g0 + j
            at = pl.ds(pl.multiple_of(g * 16, 16), 16)
            for k in range(FPD):
                for part in range(2):
                    hi, lo = split(load(base + g * BLOCK + (2 * k + part) * 16))
                    lanes = pl.ds(part * 128, 128)
                    ahi[k, at, lanes] = hi
                    alo[k, at, lanes] = lo
            return carry

        lax.fori_loop(0, n, one, 0)

    def right(q, slot, bhi, blo):
        for b in range(8):
            for k in range(FPD):
                start = (q * 8 + b) * BLOCK + 2 * k * 16
                for part in range(2):
                    value = load(start + part * 16) * SCALE
                    for ref, v in zip((bhi, blo), split(value)):
                        i = slot * FPD + k
                        ref[i, pl.ds(part * 128 + b * 16, 16), pl.ds(0, 128)] = (
                            v if part == 0 else -v
                        )
                        ref[i, pl.ds((1 - part) * 128 + b * 16, 16), pl.ds(128, 128)] = v

    def multiply(slot, row0, sizes, ahi, alo, bhi, blo, first=False):
        for k in range(FPD):
            row = row0
            for size in sizes:
                at = pl.ds(row if isinstance(row, int) else pl.multiple_of(row, 32), size)
                i = slot * FPD + k
                got = sum(
                    jnp.dot(a[k, at, :], b[i], preferred_element_type=jnp.float32)
                    for a, b in ((ahi, bhi), (alo, bhi), (ahi, blo))
                )
                for part in range(2):
                    piece = got[:, part * 128 : (part + 1) * 128]
                    if first:
                        out[part, k, at, :] = piece
                    else:
                        out[part, k, at, :] += piece
                row = row + size

    mid = zl // 2
    swap = (zl == 2) | (zl == 4)

    def near_chunk(i):
        return h * 4 + mid + (near(i, mid, 4) if i else 0)

    def far_chunk(i):
        step = near(i, mid, 4) if i else 0
        if i in (1, 2):
            step = jnp.where(swap, near(3 - i, mid, 4), step)
        if i < 2:
            step = jnp.where(zl == 2, 0 if i else near(2, mid, 4), step)
        return (1 - h) * 4 + mid + step

    def arrive(q):
        for k in range(2):
            wait(rows((2 * q + k) * GROUP, GROUP), zsem.at[2 * q + k])

    def forward():
        with jax.named_scope("relay"):
            for part in range(2):
                wait(relay.at[pl.ds(part * 2 * BLOCK, 2 * BLOCK)], rsem.at[part])
                onward(part)
                onward(part + 2)

    for i in range(7):
        take(i)
        if i:
            with jax.named_scope(f"pass{i - 1}"):
                pass_on(i - 1)
    with jax.named_scope("pass6"):
        pass_on(6)
        for i in range(7):
            from_core(i)

    ahead = [near_chunk(i) for i in range(3)] + [far_chunk(3), far_chunk(2)]
    upper = jnp.where(zl >= 4, 1, 0)
    for slot, q in enumerate(ahead):
        with jax.named_scope(f"ahead{slot}"):
            if slot >= 3:
                arrive(q)
            left(q, upper * 4, 28, ahi, alo)
            right(q, slot, bhi, blo)
            multiply(slot, upper * 64, (224, 224), ahi, alo, bhi, blo, slot == 0)
    with jax.named_scope("core"):
        far_at = place(7)

        def piece(base, dx):
            return rows(base + far_at * GROUP + lax.rem(x - dx + 4, 4) * BLOCK, BLOCK)

        for dx in range(4):
            with jax.named_scope(f"own7{dx}"):
                src = piece(h * HALF, dx)
                wait(src, zsem.at[16 + lax.rem(x - dx + 4, 4)])
            for dy in (1, 3, 2):
                send(
                    src,
                    piece(ROW + r * HALF, dx),
                    ysend,
                    ysem.at[24 + dy * 4 + dx],
                    device(0, dy, 0, 0),
                )
            to = device(0, 0, 0, 1)
            send(src, piece(ROW + r * HALF, dx), csend, csem.at[32 + dx], to)
        forward()
        for dx in range(4):
            for dy in (1, 3, 2):
                ref = piece(ROW + (lax.rem(y - dy + 4, 4) * 2 + c) * HALF, dx)
                wait(ref, ysem.at[24 + dy * 4 + dx])
                send(ref, ref, csend, csem.at[32 + dy * 4 + dx], device(0, 0, 0, 1))
        for dx in range(4):
            for dy in (0, 1, 3, 2):
                q = lax.rem(y - dy + 4, 4) * 2 + 1 - c
                wait(piece(ROW + q * HALF, dx), csem.at[32 + dy * 4 + dx])
    with jax.named_scope("near3"):
        q = near_chunk(3)
        left(q, upper * 4, 28, ahi, alo)
        right(q, 5, bhi, blo)
        multiply(5, upper * 64, (224, 224), ahi, alo, bhi, blo)
    last = (1 - upper) * 28
    for slot, q in enumerate([*ahead, near_chunk(3)]):
        with jax.named_scope(f"late{slot}"):
            left(q, last, 4, ahi, alo)
            multiply(slot, last * 16, (64,), ahi, alo, bhi, blo, slot == 0)
    ends = ((1, ahi, alo), (0, nhi, nlo))
    for i, hi, lo in ends:
        with jax.named_scope(f"left{i}"):
            left(far_chunk(i), 0, 32, hi, lo)
    for i, hi, lo in ends:
        with jax.named_scope(f"wait{i}"):
            arrive(far_chunk(i))
        with jax.named_scope(f"far{i}"):
            right(far_chunk(i), 0, whi, wlo)
            multiply(0, 0, (256, 256), hi, lo, whi, wlo)
    with jax.named_scope("end"):
        wait(big.at[pl.ds(0, 63 * BLOCK)], zsend)
        wait(big.at[pl.ds(0, 4 * BLOCK)], rsend)
        wait(big.at[pl.ds(0, 3 * HALF)], ysend)
        wait(big.at[pl.ds(0, 4 * HALF)], csend)


def per_device(traces):
    table = jnp.asarray(dft_table())
    vmem = pl.BlockSpec(memory_space=pltpu.VMEM)
    dma = pltpu.SemaphoreType.DMA
    return pl.pallas_call(
        kernel,
        name="multiples",
        out_shape=jax.ShapeDtypeStruct((2, FPD, N // 2, 128), jnp.float32),
        in_specs=[pl.BlockSpec(memory_space=pltpu.HBM)] * 2,
        out_specs=vmem,
        scratch_shapes=[
            pltpu.VMEM((2048, NT), jnp.float32),
            pltpu.VMEM((2, 2 * NF, NT), jnp.bfloat16),
            pltpu.VMEM((2 * NF * 16, 128), jnp.float32),
            pltpu.VMEM((ROW + 8 * HALF, 128), jnp.float32),
            pltpu.VMEM((FPD, 512, 256), jnp.bfloat16),
            pltpu.VMEM((FPD, 512, 256), jnp.bfloat16),
            pltpu.VMEM((6 * FPD, 256, 256), jnp.bfloat16),
            pltpu.VMEM((6 * FPD, 256, 256), jnp.bfloat16),
            pltpu.VMEM((FPD, 256, 256), jnp.bfloat16),
            pltpu.VMEM((FPD, 256, 256), jnp.bfloat16),
            pltpu.VMEM((FPD, 512, 256), jnp.bfloat16),
            pltpu.VMEM((FPD, 512, 256), jnp.bfloat16),
            dma((XPART + 1,)),
            dma,
            dma,
            dma,
            dma,
            dma((20,)),
            dma((40,)),
            dma((48,)),
            pltpu.SemaphoreType.REGULAR((2, 8)),
            pltpu.VMEM((4 * BLOCK, 128), jnp.float32),
            dma((2,)),
            dma,
        ],
        compiler_params=pltpu.CompilerParams(
            collective_id=0, has_side_effects=True, vmem_limit_bytes=48 << 20
        ),
    )(
        pltpu.with_memory_space_constraint(traces.reshape(2048, NT), pltpu.HBM),
        pltpu.with_memory_space_constraint(table, pltpu.HBM),
    )


def solution(mesh):
    in_specs = (P(("src", "freq"), "rcv", None),)
    out_specs = P(None, "freq", "src", "rcv")
    return jax.shard_map(
        per_device, mesh=mesh, in_specs=in_specs, out_specs=out_specs, check_vma=False
    )
```

```python
import functools
import math

import jax
import jax.numpy as jnp
import ml_dtypes
import numpy as np
from jax import lax
from jax.experimental import pallas as pl
from jax.experimental.pallas import tpu as pltpu
from jax.sharding import PartitionSpec as P

N = 1024
NT = 256
NF = 96
FPD = 3
PLANES = 2 * FPD
BLOCK = 16 * PLANES
GROUP = 4 * BLOCK
HALF = 8 * GROUP
ROW = 2 * HALF
MESH = pl.DeviceIdType.MESH
SCALE = -1.0 / math.sqrt(N)
XPART = 4
RFIRST = 6


def split(x):
    hi = x.astype(jnp.bfloat16)
    return hi, (x - hi.astype(jnp.float32)).astype(jnp.bfloat16)


def dft_table():
    phase = np.arange(NF)[:, None] * np.arange(NT)[None, :] % NT
    angle = phase * (2.0 * math.pi / NT)
    both = np.stack([np.cos(angle), -np.sin(angle)], axis=1)
    both = (both.reshape(2 * NF, NT) / math.sqrt(NT)).astype(np.float32)
    hi = both.astype(ml_dtypes.bfloat16)
    lo = (both - hi.astype(np.float32)).astype(ml_dtypes.bfloat16)
    return np.stack([hi, lo])


def near(i, at, count):
    sides = jnp.minimum(at, count - 1 - at)
    both = i <= 2 * sides
    far = jnp.where(both, (i + 1) // 2, i - sides)
    up = jnp.where(both, i % 2 == 1, at < count // 2)
    return jnp.where(up, far, -far)


def kernel(
    traces,
    table,
    out,
    xin,
    tab,
    spec,
    big,
    ahi,
    alo,
    bhi,
    blo,
    whi,
    wlo,
    nhi,
    nlo,
    xsem,
    lsem,
    zsend,
    ysend,
    csend,
    zsem,
    ysem,
    csem,
    ready,
    relay,
    rsem,
    rsend,
):
    f = lax.axis_index("freq")
    h = lax.axis_index("src")
    r = lax.axis_index("rcv")
    x, zl = lax.rem(f, 4), f // 4
    y, c = r // 2, lax.rem(r, 2)
    z = h * 8 + zl

    def device(dx, dy, dz, dc):
        x2, y2 = lax.rem(x + dx, 4), lax.rem(y + dy, 4)
        z2, c2 = lax.rem(z + dz + 16, 16), lax.rem(c + dc, 2)
        return (lax.rem(z2, 8) * 4 + x2, z2 // 8, y2 * 2 + c2)

    def rows(start, n):
        return big.at[pl.ds(pl.multiple_of(start, BLOCK), n)]

    def wait(ref, sem):
        pltpu.make_async_copy(ref, ref, sem).wait()

    def send(src, dst, ssem, rsem, to):
        pltpu.make_async_remote_copy(
            src, dst, ssem, rsem, device_id=to, device_id_type=MESH
        ).start()

    barrier = pltpu.get_barrier_semaphore()
    peers = [(dx, 0, dz, 0) for dz in (1, -1, 0) for dx in range(4) if dx or dz]
    peers += [(0, dy, 0, 0) for dy in (1, 2, 3)] + [(0, 0, 0, 1)]
    per = 2048 // XPART
    loads = [
        pltpu.make_async_copy(
            traces.at[pl.ds(k * per, per)], xin.at[pl.ds(k * per, per)], xsem.at[k]
        )
        for k in range(XPART)
    ]
    loads.append(pltpu.make_async_copy(table, tab, xsem.at[XPART]))
    with jax.named_scope("signal"):
        for p in peers:
            pl.semaphore_signal(
                barrier, inc=1, device_id=device(*p), device_id_type=MESH
            )
        for load in loads[-1:] + loads[:-1]:
            load.start()
    with jax.named_scope("dft"):
        loads[XPART].wait()
        thi, tlo = tab[0], tab[1]
        dims = (((1,), (1,)), ((), ()))
        for k in range(8):
            if k % (8 // XPART) == 0:
                loads[k // (8 // XPART)].wait()
            xhi, xlo = split(xin[pl.ds(k * 256, 256), :])
            got = sum(
                lax.dot_general(a, b, dims, preferred_element_type=jnp.float32)
                for a, b in ((thi, xhi), (tlo, xhi), (thi, xlo))
            )
            for i in range(2):
                spec[pl.ds(2 * k + i, 2 * NF, stride=16), :] = got[
                    :, i * 128 : (i + 1) * 128
                ]
    with jax.named_scope("barrier"):
        pl.semaphore_wait(barrier, len(peers))

    with jax.named_scope("issue"):
        mine = (z * 4 + x) * BLOCK

        def flag(to):
            at = to[0] // 4
            farthest = zl == jnp.where(at < 4, 7, 0)
            return jnp.where((to[1] == h) & farthest, 16 + x, z)

        def zcopy(dz, dx):
            to = device(dx, 0, dz, 0)
            src = spec.at[pl.ds(pl.multiple_of(to[0] * BLOCK, BLOCK), BLOCK)]
            send(src, rows(mine, BLOCK), zsend, zsem.at[flag(to)], to)

        own = pltpu.make_async_copy(
            spec.at[pl.ds(pl.multiple_of(f * BLOCK, BLOCK), BLOCK)],
            rows(mine, BLOCK),
            lsem,
        )
        own.start()
        for dx in (1, 2, 3):
            zcopy(0, dx)

    def spread(dz):
        for dx in range(4):
            zcopy(dz, dx)

    def via(dx):
        return 4 if dx % 2 == 0 else -4

    def halfway(dx):
        to = device(dx, 0, via(dx), 0)
        goal = device(dx, 0, 8, 0)[0]
        src = spec.at[pl.ds(pl.multiple_of(goal * BLOCK, BLOCK), BLOCK)]
        slot = relay.at[pl.ds((dx % 2 * 2 + dx // 2) * BLOCK, BLOCK)]
        send(src, slot, zsend, rsem.at[dx % 2], to)

    def onward(dx):
        to = device(0, 0, via(dx), 0)
        first = lax.rem(z - via(dx) + 16, 16)
        block = (first * 4 + lax.rem(x - dx + 4, 4)) * BLOCK
        slot = relay.at[pl.ds((dx % 2 * 2 + dx // 2) * BLOCK, BLOCK)]
        send(slot, rows(block, BLOCK), rsend, zsem.at[first], to)

    for k in range(1, 8):
        with jax.named_scope(f"ready{k}"):
            for s in range(2):
                if k > 1:
                    pl.semaphore_wait(ready.at[s, k], 1)
                if k < 7:
                    pl.semaphore_signal(
                        ready.at[s, k + 1],
                        inc=1,
                        device_id=device(0, 0, 2 * s - 1, 0),
                        device_id_type=MESH,
                    )
            if k == RFIRST:
                for dx in range(4):
                    halfway(dx)
            spread(k)
            spread(-k)
    if RFIRST == 8:
        for dx in range(4):
            halfway(dx)
    own.wait()

    def place(i):
        return zl + (near(i, zl, 8) if i else 0)

    def pass_on(i):
        at = place(i)
        for dy in (1, 3, 2):
            q = lax.rem(y - dy + 4, 4) * 2 + c
            ref = rows(ROW + q * HALF + at * GROUP, GROUP)
            wait(ref, ysem.at[(dy - 1) * 8 + at])
            send(ref, ref, csend, csem.at[dy * 8 + at], device(0, 0, 0, 1))

    def take(i):
        at = place(i)
        src = rows((h * 8 + at) * GROUP, GROUP)
        dst = rows(ROW + r * HALF + at * GROUP, GROUP)
        with jax.named_scope(f"own{i}"):
            wait(
                rows((h * 8 + at) * GROUP, GROUP if i else GROUP - BLOCK),
                zsem.at[h * 8 + at],
            )
        for dy in (1, 3, 2):
            send(src, dst, ysend, ysem.at[(dy - 1) * 8 + at], device(0, dy, 0, 0))
        send(src, dst, csend, csem.at[at], device(0, 0, 0, 1))

    def from_core(i):
        at = place(i)
        for dy in range(4):
            q = lax.rem(y - dy + 4, 4) * 2 + 1 - c
            wait(rows(ROW + q * HALF + at * GROUP, GROUP), csem.at[dy * 8 + at])

    def load(start):
        return big[pl.ds(pl.multiple_of(start, 16), 16), :]

    def left(q, g0, n, ahi, alo):
        base = jnp.where(q == r, h * HALF, ROW + q * HALF)

        def one(j, carry):
            g = g0 + j
            at = pl.ds(pl.multiple_of(g * 16, 16), 16)
            for k in range(FPD):
                for part in range(2):
                    hi, lo = split(load(base + g * BLOCK + (2 * k + part) * 16))
                    lanes = pl.ds(part * 128, 128)
                    ahi[k, at, lanes] = hi
                    alo[k, at, lanes] = lo
            return carry

        lax.fori_loop(0, n, one, 0)

    def right(q, slot, bhi, blo):
        for b in range(8):
            for k in range(FPD):
                start = (q * 8 + b) * BLOCK + 2 * k * 16
                for part in range(2):
                    value = load(start + part * 16) * SCALE
                    for ref, v in zip((bhi, blo), split(value)):
                        i = slot * FPD + k
                        ref[i, pl.ds(part * 128 + b * 16, 16), pl.ds(0, 128)] = (
                            v if part == 0 else -v
                        )
                        ref[i, pl.ds((1 - part) * 128 + b * 16, 16), pl.ds(128, 128)] = v

    def multiply(slot, row0, sizes, ahi, alo, bhi, blo, first=False):
        for k in range(FPD):
            row = row0
            for size in sizes:
                at = pl.ds(row if isinstance(row, int) else pl.multiple_of(row, 32), size)
                i = slot * FPD + k
                got = sum(
                    jnp.dot(a[k, at, :], b[i], preferred_element_type=jnp.float32)
                    for a, b in ((ahi, bhi), (alo, bhi), (ahi, blo))
                )
                for part in range(2):
                    piece = got[:, part * 128 : (part + 1) * 128]
                    if first:
                        out[part, k, at, :] = piece
                    else:
                        out[part, k, at, :] += piece
                row = row + size

    mid = zl // 2
    swap = (zl == 2) | (zl == 4)

    def near_chunk(i):
        return h * 4 + mid + (near(i, mid, 4) if i else 0)

    def far_chunk(i):
        step = near(i, mid, 4) if i else 0
        if i in (1, 2):
            step = jnp.where(swap, near(3 - i, mid, 4), step)
        if i < 2:
            step = jnp.where(zl == 2, 0 if i else near(2, mid, 4), step)
        return (1 - h) * 4 + mid + step

    def arrive(q):
        for k in range(2):
            wait(rows((2 * q + k) * GROUP, GROUP), zsem.at[2 * q + k])

    def forward():
        with jax.named_scope("relay"):
            for part in range(2):
                wait(relay.at[pl.ds(part * 2 * BLOCK, 2 * BLOCK)], rsem.at[part])
                onward(part)
                onward(part + 2)

    for i in range(7):
        take(i)
        if i:
            with jax.named_scope(f"pass{i - 1}"):
                pass_on(i - 1)
    with jax.named_scope("pass6"):
        pass_on(6)
        for i in range(7):
            from_core(i)

    ahead = [near_chunk(i) for i in range(3)] + [far_chunk(3), far_chunk(2)]
    upper = jnp.where(zl >= 4, 1, 0)
    for slot, q in enumerate(ahead):
        with jax.named_scope(f"ahead{slot}"):
            if slot >= 3:
                arrive(q)
            left(q, upper * 4, 28, ahi, alo)
            right(q, slot, bhi, blo)
            multiply(slot, upper * 64, (224, 224), ahi, alo, bhi, blo, slot == 0)
    with jax.named_scope("core"):
        far_at = place(7)

        def piece(base, dx):
            return rows(base + far_at * GROUP + lax.rem(x - dx + 4, 4) * BLOCK, BLOCK)

        for dx in range(4):
            with jax.named_scope(f"own7{dx}"):
                src = piece(h * HALF, dx)
                wait(src, zsem.at[16 + lax.rem(x - dx + 4, 4)])
            for dy in (1, 3, 2):
                send(
                    src,
                    piece(ROW + r * HALF, dx),
                    ysend,
                    ysem.at[24 + dy * 4 + dx],
                    device(0, dy, 0, 0),
                )
            to = device(0, 0, 0, 1)
            send(src, piece(ROW + r * HALF, dx), csend, csem.at[32 + dx], to)
        forward()
        for dx in range(4):
            for dy in (1, 3, 2):
                ref = piece(ROW + (lax.rem(y - dy + 4, 4) * 2 + c) * HALF, dx)
                wait(ref, ysem.at[24 + dy * 4 + dx])
                send(ref, ref, csend, csem.at[32 + dy * 4 + dx], device(0, 0, 0, 1))
        for dx in range(4):
            for dy in (0, 1, 3, 2):
                q = lax.rem(y - dy + 4, 4) * 2 + 1 - c
                wait(piece(ROW + q * HALF, dx), csem.at[32 + dy * 4 + dx])
    with jax.named_scope("near3"):
        q = near_chunk(3)
        left(q, upper * 4, 28, ahi, alo)
        right(q, 5, bhi, blo)
        multiply(5, upper * 64, (224, 224), ahi, alo, bhi, blo)
    last = (1 - upper) * 28
    for slot, q in enumerate([*ahead, near_chunk(3)]):
        with jax.named_scope(f"late{slot}"):
            left(q, last, 4, ahi, alo)
            multiply(slot, last * 16, (64,), ahi, alo, bhi, blo, slot == 0)
    ends = ((1, ahi, alo), (0, nhi, nlo))
    for i, hi, lo in ends:
        with jax.named_scope(f"left{i}"):
            left(far_chunk(i), 0, 32, hi, lo)
    for i, hi, lo in ends:
        with jax.named_scope(f"wait{i}"):
            arrive(far_chunk(i))
        with jax.named_scope(f"far{i}"):
            right(far_chunk(i), 0, whi, wlo)
            multiply(0, 0, (512,), hi, lo, whi, wlo)
    with jax.named_scope("end"):
        wait(big.at[pl.ds(0, 63 * BLOCK)], zsend)
        wait(big.at[pl.ds(0, 4 * BLOCK)], rsend)
        wait(big.at[pl.ds(0, 3 * HALF)], ysend)
        wait(big.at[pl.ds(0, 4 * HALF)], csend)


def per_device(traces):
    table = jnp.asarray(dft_table())
    vmem = pl.BlockSpec(memory_space=pltpu.VMEM)
    dma = pltpu.SemaphoreType.DMA
    return pl.pallas_call(
        kernel,
        name="multiples",
        out_shape=jax.ShapeDtypeStruct((2, FPD, N // 2, 128), jnp.float32),
        in_specs=[pl.BlockSpec(memory_space=pltpu.HBM)] * 2,
        out_specs=vmem,
        scratch_shapes=[
            pltpu.VMEM((2048, NT), jnp.float32),
            pltpu.VMEM((2, 2 * NF, NT), jnp.bfloat16),
            pltpu.VMEM((2 * NF * 16, 128), jnp.float32),
            pltpu.VMEM((ROW + 8 * HALF, 128), jnp.float32),
            pltpu.VMEM((FPD, 512, 256), jnp.bfloat16),
            pltpu.VMEM((FPD, 512, 256), jnp.bfloat16),
            pltpu.VMEM((6 * FPD, 256, 256), jnp.bfloat16),
            pltpu.VMEM((6 * FPD, 256, 256), jnp.bfloat16),
            pltpu.VMEM((FPD, 256, 256), jnp.bfloat16),
            pltpu.VMEM((FPD, 256, 256), jnp.bfloat16),
            pltpu.VMEM((FPD, 512, 256), jnp.bfloat16),
            pltpu.VMEM((FPD, 512, 256), jnp.bfloat16),
            dma((XPART + 1,)),
            dma,
            dma,
            dma,
            dma,
            dma((20,)),
            dma((40,)),
            dma((48,)),
            pltpu.SemaphoreType.REGULAR((2, 8)),
            pltpu.VMEM((4 * BLOCK, 128), jnp.float32),
            dma((2,)),
            dma,
        ],
        compiler_params=pltpu.CompilerParams(
            collective_id=0, has_side_effects=True, vmem_limit_bytes=48 << 20
        ),
    )(
        pltpu.with_memory_space_constraint(traces.reshape(2048, NT), pltpu.HBM),
        pltpu.with_memory_space_constraint(table, pltpu.HBM),
    )


def solution(mesh):
    in_specs = (P(("src", "freq"), "rcv", None),)
    out_specs = P(None, "freq", "src", "rcv")
    return jax.shard_map(
        per_device, mesh=mesh, in_specs=in_specs, out_specs=out_specs, check_vma=False
    )
```
